32 devices in a mesh: fsdp: 2 (over y), ctx: 4 (over z), tp: 4 (over x, core).
Axes of the slice: x: 2, y: 2, z: 4, core: 2. Of those that a mesh axis runs over, the one named last changes fastest.
Arguments:
- hidden_in: bfloat16 [2, 1024, 576], P('fsdp', 'ctx'), may hold values from -6 to 6
- segments: int32 [2, 1024], P('fsdp', 'ctx'), may hold values from 0 to 4, as said below
- positions: int32 [2, 1024], P('fsdp', 'ctx'), may hold values from 0 to 511, as said below
- attn_gain: bfloat16 [576], P('fsdp')
- query_weight: bfloat16 [576, 576], P('fsdp'), may hold values from -0.25 to 0.25
- kv_weight: bfloat16 [576, 384], P('fsdp'), may hold values from -0.25 to 0.25
- out_weight: bfloat16 [576, 576], P('fsdp'), may hold values from -1 to 1
- mlp_gain: bfloat16 [576], P('fsdp'), may hold values from 0.25 to 1.75
- gate_up_weight: bfloat16 [576, 2, 1536], P('fsdp', None, 'tp'), may hold values from -0.25 to 0.25
- down_weight: bfloat16 [576, 1536], P('fsdp', 'tp'), may hold values from -0.15625 to 0.15625
- cotangent: bfloat16 [2, 1024, 576], P('fsdp', 'ctx'), may hold values from -6 to 6
Outputs:
- block_output: bfloat16 [2, 1024, 576], P('fsdp', 'ctx')
- input_grad: float32 [2, 1024, 576], P('fsdp', 'ctx')
- attn_gain_grad: float32 [576], P('fsdp')
- query_weight_grad: float32 [576, 576], P('fsdp')
- kv_weight_grad: float32 [576, 384], P('fsdp')
- out_weight_grad: float32 [576, 576], P('fsdp')
- mlp_gain_grad: float32 [576], P('fsdp')
- gate_up_weight_grad: float32 [576, 2, 1536], P('fsdp', None, 'tp')
- down_weight_grad: float32 [576, 1536], P('fsdp', 'tp')
The draws below stay inside these ranges and needn't reach their ends.
Inputs may be any that keep to these rules, and one draw needn't show every extreme that they name: `segments`: each sequence holds 2 to 5 documents, numbered from 0 in order and filling the whole sequence; the segment number never falls and rises by at most one from one token to the next; each document has 102 tokens or more. `positions`: each token's position is the number of tokens before it in its own segment of its sequence; every sequence has a document of exactly 512 tokens, and none is longer.
All inputs are finite; a program needn't handle non-finite values.
Results may differ from the reference program's by a relative error of at most 0.02.
The reference program's roundings to bfloat16 on the way count: a program that leaves them out, or rounds other values in their place, can miss the bound.
Values may be sent and summed in bfloat16 or wider, within the bound.
A program may use at most 64 MiB of HBM per device.

```python
import jax
import jax.numpy as jnp
from jax import lax

D = 576
H = 9
KV = 3
HD = 64
FF = 1536
LEN = 1024
SEQS = 2


def document_layout(key):
    half_len = LEN // 2
    least_len = LEN // 10
    piece_count = jax.random.randint(jax.random.fold_in(key, 11), (SEQS,), 1, 5).astype(jnp.int32)
    forced_seq = jax.random.randint(jax.random.fold_in(key, 12), (), 0, SEQS).astype(jnp.int32)
    piece_count = jnp.where(jnp.arange(SEQS, dtype=jnp.int32) == forced_seq, 4, piece_count).astype(jnp.int32)
    slack = (half_len - piece_count * least_len).astype(jnp.int32)
    cuts = jax.random.randint(jax.random.fold_in(key, 13), (SEQS, 3), 0, slack[:, None] + 1).astype(jnp.int32)
    cuts = jnp.sort(cuts, axis=1)
    cut_slot = jnp.arange(3, dtype=jnp.int32)[None, :]
    cuts = jnp.where(cut_slot >= piece_count[:, None] - 1, slack[:, None], cuts).astype(jnp.int32)
    bounds = jnp.concatenate([jnp.zeros((SEQS, 1), jnp.int32), cuts, slack[:, None]], axis=1)
    piece_slot = jnp.arange(4, dtype=jnp.int32)[None, :]
    piece_len = (bounds[:, 1:] - bounds[:, :-1] + least_len * (piece_slot < piece_count[:, None]).astype(jnp.int32)).astype(jnp.int32)
    long_at = jax.random.randint(jax.random.fold_in(key, 14), (SEQS,), 0, piece_count + 1).astype(jnp.int32)
    doc_slot = jnp.arange(5, dtype=jnp.int32)[None, :]
    before = jnp.take_along_axis(piece_len, jnp.clip(doc_slot, 0, 3) + jnp.zeros((SEQS, 1), jnp.int32), axis=1)
    after = jnp.take_along_axis(piece_len, jnp.clip(doc_slot - 1, 0, 3) + jnp.zeros((SEQS, 1), jnp.int32), axis=1)
    lengths = jnp.where(doc_slot < long_at[:, None], before, jnp.where(doc_slot == long_at[:, None], half_len, after)).astype(jnp.int32)
    doc_starts = (jnp.cumsum(lengths, axis=1) - lengths).astype(jnp.int32)
    active = doc_slot < piece_count[:, None] + 1
    column = jnp.arange(LEN, dtype=jnp.int32)[None, :, None]
    begun = (column >= doc_starts[:, None, :]) & active[:, None, :]
    segment_ids = (jnp.sum(begun.astype(jnp.int32), axis=2) - 1).astype(jnp.int32)
    doc_begin = jnp.max(jnp.where(begun, doc_starts[:, None, :], 0), axis=2).astype(jnp.int32)
    return (segment_ids, (column[:, :, 0] - doc_begin).astype(jnp.int32))


def draw_segments(key, part):
    return document_layout(key)[0]


def draw_positions(key, part):
    return document_layout(key)[1]


def draw_attn_gain(key, part):
    unit_draw = jax.random.uniform(jax.random.fold_in(key, 5), (D,), jnp.float32)
    return (0.5 + unit_draw).astype(jnp.bfloat16)


def block_levels(own_key, dims, split, low, high):
    level = 1.0
    for position, parts in split:
        draws = jax.random.uniform(jax.random.fold_in(jax.random.fold_in(own_key, 6), position), (parts,), jnp.float32, low / len(split), high / len(split))
        level = level * jnp.repeat(jnp.exp(draws), dims[position] // parts).reshape((-1,) + (1,) * (len(dims) - 1 - position))
    return level


def scatter_about(stream_key, extent, spread, reach, pieces=(), held_as=jnp.bfloat16):
    gain = block_levels(stream_key, extent, pieces, -0.22, 0.18) if pieces else 1.0
    array = jax.random.normal(stream_key, extent, jnp.float32) * spread * gain
    return jnp.minimum(jnp.maximum(array, -reach), reach).astype(held_as)


def setup_inputs(seed: int = 0) -> dict:
    key_list = jax.random.split(jax.random.key(seed), 12)
    hidden_in = scatter_about(key_list[0], (SEQS, LEN, D), 1.0, 6.0, ((0, 2), (1, 4)))
    segments = draw_segments(jax.random.fold_in(key_list[11], 71), 0)
    positions = draw_positions(jax.random.fold_in(key_list[11], 71), 0)
    attn_gain = draw_attn_gain(jax.random.fold_in(key_list[11], 71), 0)
    query_weight = scatter_about(key_list[4], (D, H * HD), D ** -0.5, 0.25, ((0, 2),))
    kv_weight = scatter_about(key_list[5], (D, 2 * KV * HD), D ** -0.5, 0.25, ((0, 2),))
    out_weight = scatter_about(key_list[6], (H * HD, D), (H * HD // 16) ** -0.5, 1.0, ((0, 2),))
    mlp_gain = jnp.clip(1.0 + 0.15 * jax.random.normal(key_list[7], (D,), jnp.float32), 0.25, 1.75).astype(jnp.bfloat16)
    gate_up_weight = scatter_about(key_list[8], (D, 2, FF), D ** -0.5, 0.25, ((0, 2), (2, 4)))
    down_weight = scatter_about(key_list[9], (D, FF), FF ** -0.5, 0.15625, ((0, 2), (1, 4)))
    cotangent = scatter_about(key_list[10], (SEQS, LEN, D), 1.0, 6.0, ((0, 2), (1, 4)))
    return {"hidden_in": hidden_in, "segments": segments, "positions": positions, "attn_gain": attn_gain, "query_weight": query_weight, "kv_weight": kv_weight, "out_weight": out_weight, "mlp_gain": mlp_gain, "gate_up_weight": gate_up_weight, "down_weight": down_weight, "cotangent": cotangent}


eps = 1e-05
theta = 100000.0
neg_fill = -1e+30

def rounded(tensor):
    return lax.optimization_barrier(tensor.astype(jnp.bfloat16)).astype(jnp.float32)

def product(form, left_side, right_side):
    return jnp.einsum(form, left_side.astype(jnp.float32), right_side.astype(jnp.float32), precision=lax.Precision.HIGHEST)

def rotary_tables(doc_positions):
    freq_index = jnp.arange(HD // 2, dtype=jnp.float32)
    inverse_freq = theta ** (-2.0 * freq_index / HD)
    angles = doc_positions.astype(jnp.float32)[:, None] * inverse_freq[None, :]
    return (jnp.cos(angles)[:, None, :], jnp.sin(angles)[:, None, :])

def rotate(tensor, cos_table, sin_table):
    lower_half = tensor[..., :HD // 2]
    upper_half = tensor[..., HD // 2:]
    return jnp.concatenate([lower_half * cos_table - upper_half * sin_table, upper_half * cos_table + lower_half * sin_table], axis=-1)

def unrotate(tensor, cos_table, sin_table):
    lower_half = tensor[..., :HD // 2]
    upper_half = tensor[..., HD // 2:]
    return jnp.concatenate([lower_half * cos_table + upper_half * sin_table, upper_half * cos_table - lower_half * sin_table], axis=-1)

def norm_forward(stream, gain_row):
    inv_rms = lax.rsqrt(lax.optimization_barrier(jnp.mean(stream * stream, axis=-1, keepdims=True)) + eps)
    return (inv_rms, stream * inv_rms * gain_row.astype(jnp.float32))

def norm_backward(stream, inv_rms, gain_row, grad_normed):
    scaled = grad_normed * gain_row.astype(jnp.float32)
    gain_grad = lax.optimization_barrier(jnp.sum(grad_normed * stream * inv_rms, axis=0))
    stream_grad = inv_rms * scaled - stream * inv_rms ** 3 * lax.optimization_barrier(jnp.mean(scaled * stream, axis=-1, keepdims=True))
    return (gain_grad, stream_grad)

def key_layout(keys_all, values_all, key_segs):
    length = keys_all.shape[0]
    block_len = 512 if length % 512 == 0 else length
    block_count = length // block_len
    starts = jnp.arange(block_count, dtype=jnp.int32) * block_len
    return (keys_all.reshape(block_count, block_len, KV, HD), values_all.reshape(block_count, block_len, KV, HD), key_segs.reshape(block_count, block_len), starts)

def masked_scores(queries, key_block, seg_block, block_start, query_index, query_segs):
    key_index = block_start + jnp.arange(seg_block.shape[0], dtype=jnp.int32)
    visible = ((query_segs[:, None] == seg_block[None, :]) & (key_index[None, :] <= query_index[:, None]))[None, None]
    scores = product('rkgd,ckd->kgrc', queries, key_block) * HD ** (-0.5)
    return (visible, jnp.where(visible, scores, neg_fill))

def attention_forward(queries, layout, query_index, query_segs):
    key_blocks, value_blocks, seg_blocks, starts = layout
    row_count = queries.shape[0]
    groups = H // KV

    def stats_block(running, inputs):
        row_tops, totals = running
        key_block, seg_block, block_start = inputs
        visible, scores = masked_scores(queries, key_block, seg_block, block_start, query_index, query_segs)
        new_tops = jnp.maximum(row_tops, lax.optimization_barrier(jnp.max(scores, axis=-1)))
        weight_sum = lax.optimization_barrier(jnp.sum(jnp.where(visible, jnp.exp(scores - new_tops[..., None]), 0.0), axis=-1))
        return ((new_tops, totals * jnp.exp(row_tops - new_tops) + weight_sum), None)
    start_top = jnp.full((KV, groups, row_count), neg_fill, jnp.float32)
    start_total = jnp.zeros((KV, groups, row_count), jnp.float32)
    (row_tops, totals), unused = lax.scan(stats_block, (start_top, start_total), (key_blocks, seg_blocks, starts))
    log_norm = row_tops + jnp.log(totals)

    def output_block(accumulated, inputs):
        key_block, value_block, seg_block, block_start = inputs
        visible, scores = masked_scores(queries, key_block, seg_block, block_start, query_index, query_segs)
        attn_probs = rounded(jnp.where(visible, jnp.exp(scores - log_norm[..., None]), 0.0))
        return (accumulated + product('kgrc,ckd->rkgd', attn_probs, value_block), None)
    accumulated, unused = lax.scan(output_block, jnp.zeros((row_count, KV, groups, HD), jnp.float32), (key_blocks, value_blocks, seg_blocks, starts))
    return (rounded(accumulated), log_norm)

def attention_backward(queries, layout, query_index, query_segs, log_norm, grad_out, row_delta):
    key_blocks, value_blocks, seg_blocks, starts = layout
    row_count = queries.shape[0]
    groups = H // KV
    score_scale = HD ** (-0.5)

    def grad_block(grad_query, inputs):
        key_block, value_block, seg_block, block_start = inputs
        visible, scores = masked_scores(queries, key_block, seg_block, block_start, query_index, query_segs)
        attn_probs = jnp.where(visible, jnp.exp(scores - log_norm[..., None]), 0.0)
        grad_probs = product('rkgd,ckd->kgrc', grad_out, value_block)
        grad_scores = rounded(attn_probs * (grad_probs - row_delta[..., None]))
        grad_values = product('kgrc,rkgd->ckd', rounded(attn_probs), grad_out)
        grad_keys = product('kgrc,rkgd->ckd', grad_scores, queries) * score_scale
        grad_query = grad_query + product('kgrc,ckd->rkgd', grad_scores, key_block) * score_scale
        return (grad_query, (grad_keys, grad_values))
    grad_query, (grad_keys, grad_values) = lax.scan(grad_block, jnp.zeros((row_count, KV, groups, HD), jnp.float32), (key_blocks, value_blocks, seg_blocks, starts))
    return (grad_query, grad_keys.reshape(-1, KV, HD), grad_values.reshape(-1, KV, HD))

def reference(hidden_in, segments, positions, attn_gain, query_weight, kv_weight, out_weight, mlp_gain, gate_up_weight, down_weight, cotangent):
    groups = H // KV

    def one_sequence(totals, inputs):
        stream_b, query_segs, doc_pos, grad_top = inputs
        length = stream_b.shape[0]
        query_index = jnp.arange(length, dtype=jnp.int32)
        stream = stream_b.astype(jnp.float32)
        cos_table, sin_table = rotary_tables(doc_pos)
        inv_first, normed_first = norm_forward(stream, attn_gain)
        normed_first = rounded(normed_first)
        query_raw = product('td,dk->tk', normed_first, query_weight).reshape(length, H, HD)
        queries = rounded(rotate(query_raw, cos_table, sin_table)).reshape(length, KV, groups, HD)
        kv_raw = product('td,dk->tk', normed_first, kv_weight).reshape(length, 2, KV, HD)
        keys_all = rounded(rotate(kv_raw[:, 0], cos_table, sin_table))
        values_all = rounded(kv_raw[:, 1])
        layout = key_layout(keys_all, values_all, query_segs)
        attended, log_norm = attention_forward(queries, layout, query_index, query_segs)
        attended_flat = attended.reshape(length, H * HD)
        mid_stream = stream + product('tk,kd->td', attended_flat, out_weight)
        inv_second, normed_second = norm_forward(mid_stream, mlp_gain)
        normed_second = rounded(normed_second)
        gate_up = product('td,dcf->tcf', normed_second, gate_up_weight)
        gate_value = gate_up[:, 0]
        up_part = gate_up[:, 1]
        gate_sigmoid = jax.nn.sigmoid(gate_value)
        hidden_act = rounded(gate_value * gate_sigmoid * up_part)
        block_out = (mid_stream + product('tf,df->td', hidden_act, down_weight)).astype(jnp.bfloat16)
        grad_top_f = grad_top.astype(jnp.float32)
        down_grad = product('td,tf->df', grad_top_f, hidden_act)
        grad_hidden = product('td,df->tf', grad_top_f, down_weight)
        grad_gate = grad_hidden * up_part * gate_sigmoid * (1.0 + gate_value * (1.0 - gate_sigmoid))
        grad_up = grad_hidden * gate_value * gate_sigmoid
        grad_gu = rounded(jnp.stack([grad_gate, grad_up], axis=1))
        gate_up_grad = product('td,tcf->dcf', normed_second, grad_gu)
        grad_normed2 = product('tcf,dcf->td', grad_gu, gate_up_weight)
        mlp_gain_grad, grad_mid_norm = norm_backward(mid_stream, inv_second, mlp_gain, grad_normed2)
        grad_mid = grad_top_f + grad_mid_norm
        grad_mid_b = rounded(grad_mid)
        out_grad = product('tk,td->kd', attended_flat, grad_mid_b)
        grad_attended = rounded(product('td,kd->tk', grad_mid_b, out_weight)).reshape(length, KV, groups, HD)
        row_delta = jnp.transpose(lax.optimization_barrier(jnp.sum(grad_attended * attended, axis=-1)), (1, 2, 0))
        grad_q, grad_keys, grad_values = attention_backward(queries, layout, query_index, query_segs, log_norm, grad_attended, row_delta)
        grad_query = rounded(unrotate(grad_q.reshape(length, H, HD), cos_table, sin_table)).reshape(length, H * HD)
        grad_kv = rounded(jnp.stack([unrotate(grad_keys, cos_table, sin_table), grad_values], axis=1)).reshape(length, 2 * KV * HD)
        query_grad = product('td,tk->dk', normed_first, grad_query)
        kv_grad = product('td,tk->dk', normed_first, grad_kv)
        grad_normed1 = product('tk,dk->td', grad_query, query_weight) + product('tk,dk->td', grad_kv, kv_weight)
        attn_gain_grad, grad_in_norm = norm_backward(stream, inv_first, attn_gain, grad_normed1)
        input_grad = grad_mid + grad_in_norm
        new_terms = (attn_gain_grad, query_grad, kv_grad, out_grad, mlp_gain_grad, gate_up_grad, down_grad)
        return (jax.tree.map(jnp.add, totals, new_terms), (block_out, input_grad))
    start_totals = (jnp.zeros(attn_gain.shape, jnp.float32), jnp.zeros(query_weight.shape, jnp.float32), jnp.zeros(kv_weight.shape, jnp.float32), jnp.zeros(out_weight.shape, jnp.float32), jnp.zeros(mlp_gain.shape, jnp.float32), jnp.zeros(gate_up_weight.shape, jnp.float32), jnp.zeros(down_weight.shape, jnp.float32))
    totals, (block_outs, input_grads) = lax.scan(one_sequence, start_totals, (hidden_in, segments, positions, cotangent))
    return (block_outs, input_grads, totals[0], totals[1], totals[2], totals[3], totals[4], totals[5], totals[6])
```

```python
import functools

import jax
import jax.numpy as jnp
from jax import lax
from jax.experimental import pallas as pl
from jax.experimental.pallas import tpu as pltpu
from jax.sharding import PartitionSpec as P

HD = 64
eps = 1e-05
theta = 100000.0
BF = jnp.bfloat16
F32 = jnp.float32
MESH = pl.DeviceIdType.MESH
VM = pl.BlockSpec(memory_space=pltpu.VMEM)


def dot(a, b, ca, cb):
    return lax.dot_general(a, b, (((ca,), (cb,)), ((), ())), preferred_element_type=F32)


def greet(peers):
    barrier = pltpu.get_barrier_semaphore()
    for peer in peers:
        pl.semaphore_signal(barrier, inc=1, device_id=peer, device_id_type=MESH)
    pl.semaphore_wait(barrier, len(peers))


def ring(axis, count, offset):
    return lax.rem(lax.axis_index(axis) + (offset + count), count)


def remote(src, dst, send, recv, device):
    copy = pltpu.make_async_remote_copy(
        src_ref=src, dst_ref=dst, send_sem=send, recv_sem=recv,
        device_id=device, device_id_type=MESH,
    )
    copy.start()
    return copy


def local(src, dst, sem):
    copy = pltpu.make_async_copy(src, dst, sem)
    copy.start()
    return copy


def gather_parts(srcs, dsts, nf, send, recv, own):
    me = lax.axis_index("fsdp")
    remotes, locals_ = [], []
    for i, (src, dst) in enumerate(zip(srcs, dsts)):
        for o in range(1, nf):
            remotes.append(
                remote(src, dst.at[me], send.at[i, o], recv.at[i, o], {"fsdp": ring("fsdp", nf, o)})
            )
        locals_.append(local(src, dst.at[me], own.at[i]))
    return remotes, locals_


def finish(copies):
    for copy in copies:
        copy.wait()


def first_gather_kernel(nf, k, *refs):
    srcs, dsts = refs[:k], refs[k : 2 * k]
    send, recv, own = refs[2 * k :]
    greet([{"fsdp": ring("fsdp", nf, o)} for o in range(1, nf)])
    remotes, locals_ = gather_parts(srcs, dsts, nf, send, recv, own)
    finish(locals_)
    finish(remotes)


def first_gather(arrays, nf, cid):
    k = len(arrays)
    sems = pltpu.SemaphoreType.DMA
    return pl.pallas_call(
        functools.partial(first_gather_kernel, nf, k),
        out_shape=[jax.ShapeDtypeStruct((nf,) + a.shape, a.dtype) for a in arrays],
        in_specs=[VM] * k,
        out_specs=[VM] * k,
        scratch_shapes=[sems((k, nf)), sems((k, nf)), sems((k,))],
        compiler_params=pltpu.CompilerParams(collective_id=cid, has_side_effects=True),
        name="first_gather",
    )(*arrays)


def attend_kernel(nf, nz, back, heads, groups, q_ref, kv_ref, pos_ref, *refs):
    weights = refs[:3]
    kvw_ref, p_ref, att_ref = refs[3:6]
    full = refs[6:9]
    ksend, krecv, kown, wsend, wrecv, wown = refs[9:]
    rows = q_ref.shape[0]
    kvh = heads // groups
    greet(
        [{"ctx": ring("ctx", nz, o)} for o in range(1, nz)]
        + [{"fsdp": ring("fsdp", nf, o)} for o in range(1, nf)]
    )
    kcopies = [
        remote(kv_ref, kvw_ref.at[back - o], ksend.at[o], krecv.at[o], {"ctx": ring("ctx", nz, o)})
        for o in range(1, back + 1)
    ]
    kself = local(kv_ref, kvw_ref.at[back], kown)
    remotes, locals_ = gather_parts(weights, full, nf, wsend, wrecv, wown)
    kself.wait()
    finish(kcopies)
    window = (back + 1) * rows
    jj = lax.broadcasted_iota(jnp.int32, (rows, window), 1) - back * rows
    ii = lax.broadcasted_iota(jnp.int32, (rows, window), 0)
    visible = (jj <= ii) & (jj >= ii - pos_ref[...])
    bias = jnp.where(visible, 0.0, -1e30)
    kvw = kvw_ref[...].reshape(window, kv_ref.shape[1])
    outs = []
    for h in range(heads):
        g = h // groups
        key = kvw[:, g * HD : (g + 1) * HD]
        value = kvw[:, (kvh + g) * HD : (kvh + g + 1) * HD]
        s = dot(q_ref[:, h * HD : (h + 1) * HD], key, 1, 1) + bias
        e = jnp.exp(s - jnp.max(s, axis=1, keepdims=True))
        p = (e * (1.0 / jnp.sum(e, axis=1, keepdims=True))).astype(BF)
        p_ref[h] = p
        outs.append(dot(p, value, 1, 0).astype(BF))
    att_ref[...] = jnp.concatenate(outs, axis=1)
    finish(locals_)
    finish(remotes)


def attend(q, kv, pos, weights, nf, nz, back, heads, groups, cid):
    rows = q.shape[0]
    window = (back + 1) * rows
    sems = pltpu.SemaphoreType.DMA
    return pl.pallas_call(
        functools.partial(attend_kernel, nf, nz, back, heads, groups),
        out_shape=[
            jax.ShapeDtypeStruct((back + 1,) + kv.shape, BF),
            jax.ShapeDtypeStruct((heads, rows, window), BF),
            jax.ShapeDtypeStruct(q.shape, BF),
        ]
        + [jax.ShapeDtypeStruct((nf,) + a.shape, a.dtype) for a in weights],
        in_specs=[VM] * 6,
        out_specs=[VM] * 6,
        scratch_shapes=[
            sems((back + 1,)), sems((back + 1,)), sems(()),
            sems((3, nf)), sems((3, nf)), sems((3,)),
        ],
        compiler_params=pltpu.CompilerParams(collective_id=cid, has_side_effects=True),
        name="attend",
    )(q, kv, pos, *weights)


def tp_sum_kernel(nt, x_ref, out_ref, buf, piece, send, recv, gsend, grecv, own):
    me = lax.axis_index("tp")
    greet([{"tp": ring("tp", nt, o)} for o in range(1, nt)])
    copies = [
        remote(x_ref.at[ring("tp", nt, o)], buf.at[o], send.at[o], recv.at[o],
               {"tp": ring("tp", nt, o)})
        for o in range(1, nt)
    ]
    mine = local(x_ref.at[me], buf.at[0], own)
    mine.wait()
    total = buf[0].astype(F32)
    for o in range(1, nt):
        copies[o - 1].wait()
        total = total + buf[o].astype(F32)
    piece[...] = total.astype(BF)
    copies = [
        remote(piece, out_ref.at[me], gsend.at[o], grecv.at[o], {"tp": ring("tp", nt, o)})
        for o in range(1, nt)
    ]
    local(piece, out_ref.at[me], own).wait()
    finish(copies)


def tp_sum(x, nt, cid):
    sems = pltpu.SemaphoreType.DMA
    return pl.pallas_call(
        functools.partial(tp_sum_kernel, nt),
        out_shape=jax.ShapeDtypeStruct(x.shape, x.dtype),
        in_specs=[VM],
        out_specs=VM,
        scratch_shapes=[
            pltpu.VMEM(x.shape, BF), pltpu.VMEM(x.shape[1:], BF),
            sems((nt,)), sems((nt,)), sems((nt,)), sems((nt,)), sems(()),
        ],
        compiler_params=pltpu.CompilerParams(collective_id=cid, has_side_effects=True),
        name="tp_sum",
    )(x)


def grid_offsets(nf, nz):
    return [(a, b) for a in range(nf) for b in range(nz) if (a, b) != (0, 0)]


def grid_peer(nf, nz, a, b):
    return {"fsdp": ring("fsdp", nf, a), "ctx": ring("ctx", nz, b)}


def attend_back_kernel(nf, nz, back, heads, groups, *refs):
    q_ref, kvw_ref, p_ref, att_ref, go_ref, g1_ref, g2_ref = refs[:7]
    dq_ref, dkv_ref, s1_ref, s2_ref = refs[7:11]
    dw_buf, rk_buf, b1, b2, ssem, rsem, own, ksend, krecv = refs[11:]
    rows = q_ref.shape[0]
    kvh = heads // groups
    offsets = grid_offsets(nf, nz)
    greet([grid_peer(nf, nz, a, b) for a, b in offsets])
    me = lax.axis_index("fsdp") * nz + lax.axis_index("ctx")
    copies = []
    for i, (src, buf) in enumerate(((g1_ref, b1), (g2_ref, b2))):
        for a, b in offsets:
            target = ring("fsdp", nf, a) * nz + ring("ctx", nz, b)
            slot = a * nz + b
            copies.append(
                remote(src.at[target], buf.at[slot], ssem.at[i, slot], rsem.at[i, slot],
                       grid_peer(nf, nz, a, b))
            )
    mine = [local(g1_ref.at[me], b1.at[0], own.at[0]), local(g2_ref.at[me], b2.at[0], own.at[1])]
    window = (back + 1) * rows
    kvw = kvw_ref[...].reshape(window, kvw_ref.shape[2])
    dks, dvs, dqs = [], [], []
    for g in range(kvh):
        key = kvw[:, g * HD : (g + 1) * HD]
        value = kvw[:, (kvh + g) * HD : (kvh + g + 1) * HD]
        dk = jnp.zeros((window, HD), F32)
        dv = jnp.zeros((window, HD), F32)
        for h in range(g * groups, (g + 1) * groups):
            q = q_ref[:, h * HD : (h + 1) * HD]
            go = go_ref[:, h * HD : (h + 1) * HD]
            att = att_ref[:, h * HD : (h + 1) * HD]
            delta = jnp.sum(go.astype(F32) * att.astype(F32), axis=1, keepdims=True)
            p = p_ref[h]
            ds = (p.astype(F32) * (dot(go, value, 1, 1) - delta)).astype(BF)
            dv = dv + dot(p, go, 0, 0)
            dk = dk + dot(ds, q, 0, 0)
            dqs.append(dot(ds, key, 1, 0))
        dks.append(dk)
        dvs.append(dv)
    dkv = jnp.concatenate(dks + dvs, axis=1).reshape(back + 1, rows, 2 * kvh * HD)
    dw_buf[...] = dkv[:back].astype(BF)
    kcopies = [
        remote(dw_buf.at[back - o], rk_buf.at[o - 1], ksend.at[o], krecv.at[o],
               {"ctx": ring("ctx", nz, -o)})
        for o in range(1, back + 1)
    ]
    dq_ref[...] = jnp.concatenate(dqs, axis=1) * HD ** (-0.5)
    finish(mine)
    finish(kcopies)
    total = dkv[back]
    for o in range(back):
        total = total + rk_buf[o].astype(F32)
    dkv_ref[...] = total
    finish(copies)
    for buf, out in ((b1, s1_ref), (b2, s2_ref)):
        total = buf[0].astype(F32)
        for i in range(1, nf * nz):
            total = total + buf[i].astype(F32)
        out[...] = total.astype(BF)


def attend_back(q, kvw, p, att, go, g1, g2, nf, nz, back, heads, groups, cid):
    rows = q.shape[0]
    sems = pltpu.SemaphoreType.DMA
    n = nf * nz
    return pl.pallas_call(
        functools.partial(attend_back_kernel, nf, nz, back, heads, groups),
        out_shape=[
            jax.ShapeDtypeStruct(q.shape, F32),
            jax.ShapeDtypeStruct(kvw.shape[1:], F32),
            jax.ShapeDtypeStruct(g1.shape[1:], BF),
            jax.ShapeDtypeStruct(g2.shape[1:], BF),
        ],
        in_specs=[VM] * 7,
        out_specs=[VM] * 4,
        scratch_shapes=[
            pltpu.VMEM((back,) + kvw.shape[1:], BF), pltpu.VMEM((back,) + kvw.shape[1:], BF),
            pltpu.VMEM(g1.shape, BF), pltpu.VMEM(g2.shape, BF),
            sems((2, n)), sems((2, n)), sems((2,)), sems((back + 1,)), sems((back + 1,)),
        ],
        compiler_params=pltpu.CompilerParams(collective_id=cid, has_side_effects=True),
        name="attend_back",
    )(q, kvw, p, att, go, g1, g2)


def last_sum_kernel(nf, nz, nt, *refs):
    w_ref, v_ref, s1_ref, s2_ref, out_ref, vout_ref, o1_ref, o2_ref = refs[:8]
    buf, vbuf, piece, vpiece, ssem, rsem, own, gsend, grecv, tsend, trecv = refs[8:]
    offsets = grid_offsets(nf, nz)
    z = lax.axis_index("ctx")
    cols = piece.shape[1]
    columns = pl.ds(pl.multiple_of(lax.axis_index("tp") * cols, cols), cols)
    greet(
        [grid_peer(nf, nz, a, b) for a, b in offsets]
        + [{"tp": ring("tp", nt, o)} for o in range(1, nt)]
    )
    me = lax.axis_index("fsdp") * nz + z
    copies = []
    for a, b in offsets:
        target = ring("fsdp", nf, a) * nz + ring("ctx", nz, b)
        slot = a * nz + b
        peer = grid_peer(nf, nz, a, b)
        copies.append(
            remote(w_ref.at[target, :, columns], buf.at[slot], ssem.at[0, slot], rsem.at[0, slot], peer)
        )
        copies.append(
            remote(v_ref.at[target], vbuf.at[slot], ssem.at[1, slot], rsem.at[1, slot], peer)
        )
    mine = [
        local(w_ref.at[me, :, columns], buf.at[0], own.at[0]),
        local(v_ref.at[me], vbuf.at[0], own.at[1]),
        local(s1_ref, o1_ref.at[z], own.at[2]),
        local(s2_ref, o2_ref.at[z], own.at[3]),
    ]
    gathers = []
    for i, (src, dst) in enumerate(((s1_ref, o1_ref), (s2_ref, o2_ref))):
        for o in range(1, nz):
            gathers.append(
                remote(src, dst.at[z], gsend.at[i, o], grecv.at[i, o], {"ctx": ring("ctx", nz, o)})
            )
    finish(mine)
    finish(copies)
    for source, target in ((buf, piece), (vbuf, vpiece)):
        total = source[0].astype(F32)
        for i in range(1, nf * nz):
            total = total + source[i].astype(F32)
        target[...] = total.astype(target.dtype)
    late = []
    for i, (src, dst) in enumerate(
        ((piece, out_ref.at[z, :, columns]), (vpiece, vout_ref.at[z]))
    ):
        for o in range(1, nz):
            late.append(
                remote(src, dst, gsend.at[2 + i, o], grecv.at[2 + i, o], {"ctx": ring("ctx", nz, o)})
            )
        local(src, dst, own.at[i]).wait()
    finish(late)
    part = out_ref.at[:, :, columns]
    finish(
        [
            remote(part, part, tsend.at[o], trecv.at[o], {"tp": ring("tp", nt, o)})
            for o in range(1, nt)
        ]
    )
    finish(gathers)


def last_sum(w, v, s1, s2, nf, nz, nt, cid):
    sems = pltpu.SemaphoreType.DMA
    n, rows, cols = w.shape
    part = cols // nt
    return pl.pallas_call(
        functools.partial(last_sum_kernel, nf, nz, nt),
        out_shape=[
            jax.ShapeDtypeStruct((nz, rows, cols), BF),
            jax.ShapeDtypeStruct((nz,) + v.shape[1:], F32),
            jax.ShapeDtypeStruct((nz,) + s1.shape, BF),
            jax.ShapeDtypeStruct((nz,) + s2.shape, BF),
        ],
        in_specs=[VM] * 4,
        out_specs=[VM] * 4,
        scratch_shapes=[
            pltpu.VMEM((n, rows, part), BF), pltpu.VMEM(v.shape, F32),
            pltpu.VMEM((rows, part), BF), pltpu.VMEM(v.shape[1:], F32),
            sems((2, n)), sems((2, n)), sems((4,)),
            sems((4, nz)), sems((4, nz)), sems((nt,)), sems((nt,)),
        ],
        compiler_params=pltpu.CompilerParams(collective_id=cid, has_side_effects=True),
        name="last_sum",
    )(w, v, s1, s2)


def swap_halves(x):
    width = x.shape[1]
    lane = lax.broadcasted_iota(jnp.int32, x.shape, 1) % HD
    half = HD // 2
    return jnp.where(lane < half, jnp.roll(x, -half, axis=1), jnp.roll(x, half, axis=1))


def rotary(pos, count, plain):
    freq = theta ** (-2.0 * jnp.arange(HD // 2, dtype=F32) / HD)
    angles = pos.astype(F32)[:, None] * freq[None, :]
    cos, sin = jnp.cos(angles), jnp.sin(angles)
    rows = pos.shape[0]
    c = jnp.tile(jnp.concatenate([cos, cos], axis=1), (1, count))
    s = jnp.tile(jnp.concatenate([-sin, sin], axis=1), (1, count))
    return (
        jnp.concatenate([c, jnp.ones((rows, plain), F32)], axis=1),
        jnp.concatenate([s, jnp.zeros((rows, plain), F32)], axis=1),
    )


def inverse_rms(x):
    return lax.rsqrt(jnp.mean(x * x, axis=-1, keepdims=True) + eps)


def norm_back(x, inv, gain, grad):
    scaled = grad * gain
    gain_grad = jnp.sum(grad * x * inv, axis=0)
    return gain_grad, inv * scaled - x * inv**3 * jnp.mean(scaled * x, axis=-1, keepdims=True)


def shards(nf, nz, nt, hidden_in, segments, positions, attn_gain, query_weight, kv_weight,
           out_weight, mlp_gain, gate_up_weight, down_weight, cotangent):
    rows, d = hidden_in.shape[1:]
    heads = query_weight.shape[1] // HD
    kvh = kv_weight.shape[1] // (2 * HD)
    groups = heads // kvh
    dq, dkv = heads * HD, 2 * kvh * HD
    ff = down_weight.shape[1]
    span = rows * nz // 2
    back = min(nz - 1, -(-(span - 1) // rows))
    x = hidden_in.reshape(rows, d).astype(F32)
    pos = positions.reshape(rows)
    top = cotangent.reshape(rows, d)

    gains, wq, wkv = first_gather(
        [jnp.stack([attn_gain, mlp_gain]), query_weight, kv_weight], nf, 1
    )
    gains = jnp.transpose(gains, (1, 0, 2)).reshape(2, d).astype(F32)
    gain1, gain2 = gains[0], gains[1]
    wqkv = jnp.concatenate([wq.reshape(d, dq), wkv.reshape(d, dkv)], axis=1)
    ctab, stab = rotary(pos, heads + kvh, kvh * HD)
    r1 = inverse_rms(x)
    n1 = (x * r1 * gain1).astype(BF)
    raw = dot(n1, wqkv, 1, 0)
    qkv = (raw * ctab + swap_halves(raw) * stab).astype(BF)
    q = qkv[:, :dq] * jnp.asarray(HD ** (-0.5), BF)
    kv = qkv[:, dq:]

    kvw, p, att, wo, wgu, wd = attend(
        q, kv, pos[:, None],
        [out_weight, gate_up_weight.reshape(-1, 2 * ff), down_weight],
        nf, nz, back, heads, groups, 2,
    )
    wo = wo.reshape(dq, d)
    wgu = wgu.reshape(d, 2 * ff)
    wd = wd.reshape(d, ff)
    mid = x + dot(att, wo, 1, 0)
    r2 = inverse_rms(mid)
    n2 = (mid * r2 * gain2).astype(BF)
    gu = dot(n2, wgu, 1, 0)
    gate, up = gu[:, :ff], gu[:, ff:]
    sig = jax.nn.sigmoid(gate)
    hidden = (gate * sig * up).astype(BF)
    gh = dot(top, wd, 1, 0)
    ggu = jnp.concatenate(
        [gh * up * sig * (1.0 + gate * (1.0 - sig)), gh * gate * sig], axis=1
    ).astype(BF)
    part = jnp.concatenate([dot(hidden, wd, 1, 1), dot(ggu, wgu, 1, 1)], axis=1).astype(BF)
    summed = tp_sum(part.reshape(nt, rows // nt, 2 * d), nt, 3).reshape(rows, 2 * d).astype(F32)
    block_out = (mid + summed[:, :d]).astype(BF).reshape(1, rows, d)
    n = nf * nz
    down_grad = dot(top, hidden, 0, 0).astype(BF).reshape(n, d // n, ff)
    gu_grad = dot(n2, ggu, 0, 0).astype(BF).reshape(n, d // n, 2 * ff)
    mlp_gain_grad, grad_norm = norm_back(mid, r2, gain2, summed[:, d:])
    grad_mid = top.astype(F32) + grad_norm
    grad_mid_b = grad_mid.astype(BF)
    go = dot(grad_mid_b, wo, 1, 1).astype(BF)

    grad_q, grad_kv, s1, s2 = attend_back(
        q, kvw, p, att, go, gu_grad, down_grad, nf, nz, back, heads, groups, 4
    )
    grads = jnp.concatenate([grad_q, grad_kv], axis=1)
    grads = (grads * ctab - swap_halves(grads) * stab).astype(BF)
    dw = jnp.concatenate([dot(n1, grads, 0, 0), dot(att, grad_mid_b, 0, 0)], axis=1)
    grad_n1 = dot(grads, wqkv, 1, 1)
    attn_gain_grad, grad_in = norm_back(x, r1, gain1, grad_n1)
    input_grad = (grad_mid + grad_in).reshape(1, rows, d)
    gain_grads = jnp.transpose(
        jnp.stack([attn_gain_grad, mlp_gain_grad]).reshape(2, n, d // n), (1, 0, 2)
    )
    out, gout, o1, o2 = last_sum(
        dw.astype(BF).reshape(n, d // n, -1), gain_grads, s1, s2, nf, nz, nt, 5
    )
    local_d = d // nf
    out = out.reshape(local_d, -1).astype(F32)
    gout = jnp.transpose(gout, (1, 0, 2)).reshape(2, local_d)
    return (
        block_out,
        input_grad,
        gout[0],
        out[:, :dq],
        out[:, dq : dq + dkv],
        out[:, dq + dkv :],
        gout[1],
        o1.reshape(local_d, 2, ff).astype(F32),
        o2.reshape(local_d, ff).astype(F32),
    )


def solution(mesh):
    sizes = mesh.shape
    return jax.shard_map(
        functools.partial(shards, sizes["fsdp"], sizes["ctx"], sizes["tp"]),
        mesh=mesh,
        in_specs=(
            P("fsdp", "ctx", None), P("fsdp", "ctx"), P("fsdp", "ctx"), P("fsdp"),
            P("fsdp", None), P("fsdp", None), P("fsdp", None), P("fsdp"),
            P("fsdp", None, "tp"), P("fsdp", "tp"), P("fsdp", "ctx", None),
        ),
        out_specs=(
            P("fsdp", "ctx", None), P("fsdp", "ctx", None), P("fsdp"),
            P("fsdp", None), P("fsdp", None), P("fsdp", None), P("fsdp"),
            P("fsdp", None, "tp"), P("fsdp", "tp"),
        ),
        check_vma=False,
    )
```

```python
import functools

import jax
import jax.numpy as jnp
from jax import lax
from jax.experimental import pallas as pl
from jax.experimental.pallas import tpu as pltpu
from jax.sharding import PartitionSpec as P

HD = 64
eps = 1e-05
theta = 100000.0
BF = jnp.bfloat16
F32 = jnp.float32
MESH = pl.DeviceIdType.MESH
VM = pl.BlockSpec(memory_space=pltpu.VMEM)


def dot(a, b, ca, cb):
    return lax.dot_general(a, b, (((ca,), (cb,)), ((), ())), preferred_element_type=F32)


def greet(peers):
    barrier = pltpu.get_barrier_semaphore()
    for peer in peers:
        pl.semaphore_signal(barrier, inc=1, device_id=peer, device_id_type=MESH)
    pl.semaphore_wait(barrier, len(peers))


def ring(axis, count, offset):
    return lax.rem(lax.axis_index(axis) + (offset + count), count)


def remote(src, dst, send, recv, device):
    copy = pltpu.make_async_remote_copy(
        src_ref=src, dst_ref=dst, send_sem=send, recv_sem=recv,
        device_id=device, device_id_type=MESH,
    )
    copy.start()
    return copy


def local(src, dst, sem):
    copy = pltpu.make_async_copy(src, dst, sem)
    copy.start()
    return copy


def finish(copies):
    for copy in copies:
        copy.wait()


def across(nt):
    return [{"tp": ring("tp", nt, o)} for o in range(1, nt)]


def partner():
    t = lax.axis_index("tp")
    return {"tp": t + 1 - 2 * lax.rem(t, 2)}


def attend_kernel(nf, nz, nt, back, heads, kvh, head_cols, *refs):
    x_ref, pos_ref, c_ref, s_ref, gain_ref, w_ref, gu_ref, dn_ref = refs[:8]
    n1_ref, q_ref, kvw_ref, p_ref, att_ref, fgain, fw, fgu, fdn = refs[8:17]
    ysend, yrecv, own, psend, precv, ksend, krecv, fsend, frecv = refs[17:]
    rows, d = x_ref.shape
    dq, dkv, dk = heads * HD, 2 * kvh * HD, kvh * HD
    groups = heads // kvh
    f = lax.axis_index("fsdp")
    core = lax.rem(lax.axis_index("tp"), 2)
    mate = partner()
    greet(
        [{"ctx": ring("ctx", nz, o)} for o in range(1, nz)]
        + [{"fsdp": ring("fsdp", nf, o)} for o in range(1, nf)]
        + [mate]
    )
    h1 = head_cols // 2
    h2 = (w_ref.shape[1] - head_cols) // 2
    first = pl.ds(pl.multiple_of(core * h1, 128), h1)
    second = pl.ds(pl.multiple_of(head_cols + core * h2, 128), h2)
    plans = [
        (gain_ref, fgain.at[f]),
        (w_ref.at[:, first], fw.at[f, :, first]),
        (w_ref.at[:, second], fw.at[f, :, second]),
        (dn_ref, fdn.at[f]),
        (gu_ref, fgu.at[f]),
    ]
    sent = [
        [
            remote(src, dst, ysend.at[i, o], yrecv.at[i, o], {"fsdp": ring("fsdp", nf, o)})
            for o in range(1, nf)
        ]
        for i, (src, dst) in enumerate(plans)
    ]
    mine = [
        local(src, dst.at[f], own.at[i])
        for i, (src, dst) in enumerate(
            ((gain_ref, fgain), (w_ref, fw), (dn_ref, fdn), (gu_ref, fgu))
        )
    ]

    def pass_on(i, k, columns):
        out = []
        for o in range(1, nf):
            sent[i][o - 1].wait()
            part = fw.at[ring("fsdp", nf, -o), :, columns]
            out.append(remote(part, part, psend.at[k, o], precv.at[k, o], mate))
        return out

    x = x_ref[...].astype(F32)
    normed = x * lax.rsqrt(jnp.mean(x * x, axis=1, keepdims=True) + eps)
    r = lax.broadcasted_iota(jnp.int32, (dq, dq), 0)
    c = lax.broadcasted_iota(jnp.int32, (dq, dq), 1)
    half = HD // 2
    lane = lax.rem(c, HD)
    perm = jnp.where(r == jnp.where(lane < half, c + half, c - half), 1.0, 0.0).astype(BF)
    finish(mine)
    finish(sent[0])
    finish(pass_on(1, 0, first))
    gain = jnp.concatenate([fgain[i, 0:1, :] for i in range(nf)], axis=1).astype(F32)
    n1 = (normed * gain).astype(BF)
    n1_ref[...] = n1
    w = fw[:, :, : dq + dkv].reshape(d, dq + dkv)
    wq, wk = w[:, :dq], w[:, dq : dq + dk]
    ct, st = c_ref[...], s_ref[...]
    k = dot(n1, wk, 1, 0) * ct[:, :dk] + dot(
        n1, dot(wk, perm[:dk, :dk], 1, 0).astype(BF), 1, 0
    ) * st[:, :dk]
    v = dot(n1, w[:, dq + dk :], 1, 0)
    kvw_ref[back] = jnp.concatenate([k, v], axis=1).astype(BF)
    hr = rows // 2
    block = pl.ds(pl.multiple_of(core * hr, hr), hr)
    kcopies = [
        remote(kvw_ref.at[back, block], kvw_ref.at[back - o, block], ksend.at[o], krecv.at[o],
               {"ctx": ring("ctx", nz, o)})
        for o in range(1, back + 1)
    ]
    q = dot(n1, wq, 1, 0) * ct + dot(n1, dot(wq, perm, 1, 0).astype(BF), 1, 0) * st
    q_ref[...] = (q.astype(BF).astype(F32) * HD ** (-0.5)).astype(BF)
    window = (back + 1) * rows
    jj = lax.broadcasted_iota(jnp.int32, (rows, window), 1) - back * rows
    ii = lax.broadcasted_iota(jnp.int32, (rows, window), 0)
    visible = (jj <= ii) & (jj >= ii - pos_ref[...])
    bias = jnp.where(visible, 0.0, -1e30)
    shared = []
    for o in range(1, back + 1):
        kcopies[o - 1].wait()
        part = kvw_ref.at[back - o, block]
        shared.append(remote(part, part, fsend.at[o], frecv.at[o], mate))
    finish(shared)
    kvw = kvw_ref[...].reshape(window, dkv)
    outs = []
    late = []
    for h in range(heads):
        if h == heads // 2:
            late = pass_on(2, 1, second)
        g = h // groups
        key = kvw[:, g * HD : (g + 1) * HD]
        value = kvw[:, (kvh + g) * HD : (kvh + g + 1) * HD]
        s = dot(q_ref[:, h * HD : (h + 1) * HD], key, 1, 1) + bias
        e = jnp.exp(s - jnp.max(s, axis=1, keepdims=True))
        p = (e * (1.0 / jnp.sum(e, axis=1, keepdims=True))).astype(BF)
        p_ref[h] = p
        outs.append(dot(p, value, 1, 0).astype(BF))
    att_ref[...] = jnp.concatenate(outs, axis=1)
    finish(late)
    finish(sent[3])
    finish(sent[4])


def attend(x, pos, ct, st, gains, w, gu, dn, nf, nz, nt, back, heads, kvh, head_cols, cid):
    rows, d = x.shape
    window = (back + 1) * rows
    sems = pltpu.SemaphoreType.DMA
    shape = jax.ShapeDtypeStruct
    return pl.pallas_call(
        functools.partial(attend_kernel, nf, nz, nt, back, heads, kvh, head_cols),
        out_shape=[
            shape((rows, d), BF),
            shape((rows, heads * HD), BF),
            shape((back + 1, rows, 2 * kvh * HD), BF),
            shape((heads, rows, window), BF),
            shape((rows, heads * HD), BF),
        ]
        + [shape((nf,) + a.shape, a.dtype) for a in (gains, w, gu, dn)],
        in_specs=[VM] * 8,
        out_specs=[VM] * 9,
        scratch_shapes=[
            sems((5, nf)), sems((5, nf)), sems((4,)), sems((2, nf)), sems((2, nf)),
            sems((back + 1,)), sems((back + 1,)), sems((back + 1,)), sems((back + 1,)),
        ],
        compiler_params=pltpu.CompilerParams(collective_id=cid, has_side_effects=True),
        name="attend",
    )(x, pos, ct, st, gains, w, gu, dn)


def tp_sum_kernel(nf, nt, x_ref, g1_ref, g2_ref, out_ref, o1_ref, o2_ref, buf, piece, b1, b2,
                  send, recv, gsend, grecv, own, ysend, yrecv):
    me = lax.axis_index("tp")
    f = lax.axis_index("fsdp")
    greet(across(nt) + [{"fsdp": ring("fsdp", nf, o)} for o in range(1, nf)])
    copies = [
        remote(x_ref.at[ring("tp", nt, o)], buf.at[o], send.at[o], recv.at[o],
               {"tp": ring("tp", nt, o)})
        for o in range(1, nt)
    ]
    side = [
        remote(src.at[ring("fsdp", nf, o)], dst.at[o], ysend.at[i, o], yrecv.at[i, o],
               {"fsdp": ring("fsdp", nf, o)})
        for i, (src, dst) in enumerate(((g1_ref, b1), (g2_ref, b2)))
        for o in range(1, nf)
    ]
    total = x_ref[me].astype(F32)
    for o in range(1, nt):
        copies[o - 1].wait()
        total = total + buf[o].astype(F32)
    piece[...] = total.astype(BF)
    copies = [
        remote(piece, out_ref.at[me], gsend.at[o], grecv.at[o], {"tp": ring("tp", nt, o)})
        for o in range(1, nt)
    ]
    local(piece, out_ref.at[me], own).wait()
    finish(side)
    for src, dst, out in ((g1_ref, b1, o1_ref), (g2_ref, b2, o2_ref)):
        total = src[f].astype(F32)
        for o in range(1, nf):
            total = total + dst[o].astype(F32)
        out[...] = total.astype(BF)
    finish(copies)


def tp_sum(x, g1, g2, nf, nt, cid):
    sems = pltpu.SemaphoreType.DMA
    shape = jax.ShapeDtypeStruct
    return pl.pallas_call(
        functools.partial(tp_sum_kernel, nf, nt),
        out_shape=[shape(x.shape, BF), shape(g1.shape[1:], BF), shape(g2.shape[1:], BF)],
        in_specs=[VM] * 3,
        out_specs=[VM] * 3,
        scratch_shapes=[
            pltpu.VMEM(x.shape, BF), pltpu.VMEM(x.shape[1:], BF),
            pltpu.VMEM(g1.shape, BF), pltpu.VMEM(g2.shape, BF),
            sems((nt,)), sems((nt,)), sems((nt,)), sems((nt,)), sems(()),
            sems((2, nf)), sems((2, nf)),
        ],
        compiler_params=pltpu.CompilerParams(collective_id=cid, has_side_effects=True),
        name="tp_sum",
    )(x, g1, g2)


def grid_offsets(nf, nz):
    return [(a, b) for a in range(nf) for b in range(nz) if (a, b) != (0, 0)]


def grid_peer(nf, nz, a, b):
    return {"fsdp": ring("fsdp", nf, a), "ctx": ring("ctx", nz, b)}


def attend_back_kernel(nz, nt, back, heads, groups, *refs):
    q_ref, kvw_ref, p_ref, att_ref, go_ref, g1_ref, g2_ref = refs[:7]
    dq_ref, dkv_ref, s1_ref, s2_ref = refs[7:11]
    dw_buf, rk_buf, piece, b1, b2, ssem, rsem, own, ksend, krecv, tsend, trecv = refs[11:]
    rows = q_ref.shape[0]
    kvh = heads // groups
    greet([{"ctx": ring("ctx", nz, o)} for o in range(1, nz)] + across(nt))
    me = lax.axis_index("ctx")
    copies = [
        remote(src.at[ring("ctx", nz, o)], buf.at[o], ssem.at[i, o], rsem.at[i, o],
               {"ctx": ring("ctx", nz, o)})
        for i, (src, buf) in enumerate(((g1_ref, b1), (g2_ref, b2)))
        for o in range(1, nz)
    ]
    window = (back + 1) * rows
    kvw = kvw_ref[...].reshape(window, kvw_ref.shape[2])
    dks, dvs, dqs = [], [], []
    for g in range(kvh):
        key = kvw[:, g * HD : (g + 1) * HD]
        value = kvw[:, (kvh + g) * HD : (kvh + g + 1) * HD]
        dk = jnp.zeros((window, HD), F32)
        dv = jnp.zeros((window, HD), F32)
        for h in range(g * groups, (g + 1) * groups):
            q = q_ref[:, h * HD : (h + 1) * HD]
            go = go_ref[:, h * HD : (h + 1) * HD]
            att = att_ref[:, h * HD : (h + 1) * HD]
            delta = jnp.sum(go.astype(F32) * att.astype(F32), axis=1, keepdims=True)
            p = p_ref[h]
            ds = (p.astype(F32) * (dot(go, value, 1, 1) - delta)).astype(BF)
            dv = dv + dot(p, go, 0, 0)
            dk = dk + dot(ds, q, 0, 0)
            dqs.append(dot(ds, key, 1, 0))
        dks.append(dk)
        dvs.append(dv)
    dkv = jnp.concatenate(dks + dvs, axis=1)
    quarter = rows // nt
    t = lax.axis_index("tp")
    block = pl.ds(pl.multiple_of(t * quarter, quarter), quarter)
    dw_buf[...] = dkv.reshape(back + 1, rows, 2 * kvh * HD).astype(BF)
    kcopies = [
        remote(dw_buf.at[back - o, block], rk_buf.at[o - 1], ksend.at[o], krecv.at[o],
               {"ctx": ring("ctx", nz, -o)})
        for o in range(1, back + 1)
    ]
    dq_ref[...] = jnp.concatenate(dqs, axis=1) * HD ** (-0.5)
    total = dw_buf[back, block].astype(F32)
    for o in range(back):
        kcopies[o].wait()
        total = total + rk_buf[o].astype(F32)
    piece[...] = total.astype(BF)
    tcopies = [
        remote(piece, dkv_ref.at[t], tsend.at[o], trecv.at[o], {"tp": ring("tp", nt, o)})
        for o in range(1, nt)
    ]
    local(piece, dkv_ref.at[t], own).wait()
    finish(copies)
    for src, buf, out in ((g1_ref, b1, s1_ref), (g2_ref, b2, s2_ref)):
        total = src[me].astype(F32)
        for o in range(1, nz):
            total = total + buf[o].astype(F32)
        out[...] = total.astype(BF)
    finish(tcopies)


def attend_back(q, kvw, p, att, go, g1, g2, nz, nt, back, heads, groups, cid):
    rows = q.shape[0]
    sems = pltpu.SemaphoreType.DMA
    quarter = rows // nt
    return pl.pallas_call(
        functools.partial(attend_back_kernel, nz, nt, back, heads, groups),
        out_shape=[
            jax.ShapeDtypeStruct(q.shape, F32),
            jax.ShapeDtypeStruct((nt, quarter, kvw.shape[2]), BF),
            jax.ShapeDtypeStruct(g1.shape[1:], BF),
            jax.ShapeDtypeStruct(g2.shape[1:], BF),
        ],
        in_specs=[VM] * 7,
        out_specs=[VM] * 4,
        scratch_shapes=[
            pltpu.VMEM(kvw.shape, BF), pltpu.VMEM((back, quarter, kvw.shape[2]), BF),
            pltpu.VMEM((quarter, kvw.shape[2]), BF),
            pltpu.VMEM(g1.shape, BF), pltpu.VMEM(g2.shape, BF),
            sems((2, nz)), sems((2, nz)), sems(()), sems((back + 1,)), sems((back + 1,)),
            sems((nt,)), sems((nt,)),
        ],
        compiler_params=pltpu.CompilerParams(collective_id=cid, has_side_effects=True),
        name="attend_back",
    )(q, kvw, p, att, go, g1, g2)


def last_sum_kernel(nf, nz, nt, *refs):
    w_ref, v_ref, s1_ref, s2_ref, out_ref, vout_ref, o1_ref, o2_ref = refs[:8]
    buf, vbuf, piece, vpiece, ssem, rsem, own, gsend, grecv, tsend, trecv = refs[8:]
    offsets = grid_offsets(nf, nz)
    z = lax.axis_index("ctx")
    cols = piece.shape[1]
    columns = pl.ds(pl.multiple_of(lax.axis_index("tp") * cols, cols), cols)
    greet(
        [grid_peer(nf, nz, a, b) for a, b in offsets]
        + [{"tp": ring("tp", nt, o)} for o in range(1, nt)]
    )
    me = lax.axis_index("fsdp") * nz + z
    copies = []
    for a, b in offsets:
        target = ring("fsdp", nf, a) * nz + ring("ctx", nz, b)
        slot = a * nz + b
        peer = grid_peer(nf, nz, a, b)
        copies.append(
            remote(w_ref.at[target, :, columns], buf.at[slot], ssem.at[0, slot], rsem.at[0, slot], peer)
        )
        copies.append(
            remote(v_ref.at[target], vbuf.at[slot], ssem.at[1, slot], rsem.at[1, slot], peer)
        )
    mine = [
        local(w_ref.at[me, :, columns], buf.at[0], own.at[0]),
        local(v_ref.at[me], vbuf.at[0], own.at[1]),
        local(s1_ref, o1_ref.at[z], own.at[2]),
        local(s2_ref, o2_ref.at[z], own.at[3]),
    ]
    gathers = []
    for i, (src, dst) in enumerate(((s1_ref, o1_ref), (s2_ref, o2_ref))):
        for o in range(1, nz):
            gathers.append(
                remote(src, dst.at[z], gsend.at[i, o], grecv.at[i, o], {"ctx": ring("ctx", nz, o)})
            )
    finish(mine)
    finish(copies)
    for source, target in ((buf, piece), (vbuf, vpiece)):
        total = source[0].astype(F32)
        for i in range(1, nf * nz):
            total = total + source[i].astype(F32)
        target[...] = total.astype(target.dtype)
    late = []
    for i, (src, dst) in enumerate(
        ((piece, out_ref.at[z, :, columns]), (vpiece, vout_ref.at[z]))
    ):
        for o in range(1, nz):
            late.append(
                remote(src, dst, gsend.at[2 + i, o], grecv.at[2 + i, o], {"ctx": ring("ctx", nz, o)})
            )
        local(src, dst, own.at[i]).wait()
    finish(late)
    t = lax.axis_index("tp")
    part = out_ref.at[:, :, columns]
    hops = [
        remote(part, part, tsend.at[2 * o], trecv.at[2 * o], {"tp": ring("tp", nt, 2 * o)})
        for o in range(1, nt // 2)
    ]
    swaps = [remote(part, part, tsend.at[0], trecv.at[0], partner())]
    for o in range(1, nt // 2):
        hops[o - 1].wait()
        theirs = lax.rem(t + (nt - 2 * o), nt)
        got = out_ref.at[:, :, pl.ds(pl.multiple_of(theirs * cols, cols), cols)]
        swaps.append(remote(got, got, tsend.at[2 * o + 1], trecv.at[2 * o + 1], partner()))
    finish(swaps)
    finish(gathers)


def last_sum(w, v, s1, s2, nf, nz, nt, cid):
    sems = pltpu.SemaphoreType.DMA
    n, rows, cols = w.shape
    part = cols // nt
    return pl.pallas_call(
        functools.partial(last_sum_kernel, nf, nz, nt),
        out_shape=[
            jax.ShapeDtypeStruct((nz, rows, cols), BF),
            jax.ShapeDtypeStruct((nz,) + v.shape[1:], F32),
            jax.ShapeDtypeStruct((nz,) + s1.shape, BF),
            jax.ShapeDtypeStruct((nz,) + s2.shape, BF),
        ],
        in_specs=[VM] * 4,
        out_specs=[VM] * 4,
        scratch_shapes=[
            pltpu.VMEM((n, rows, part), BF), pltpu.VMEM(v.shape, F32),
            pltpu.VMEM((rows, part), BF), pltpu.VMEM(v.shape[1:], F32),
            sems((2, n)), sems((2, n)), sems((4,)),
            sems((4, nz)), sems((4, nz)), sems((nt,)), sems((nt,)),
        ],
        compiler_params=pltpu.CompilerParams(collective_id=cid, has_side_effects=True),
        name="last_sum",
    )(w, v, s1, s2)


def swap_halves(x):
    width = x.shape[1]
    lane = lax.broadcasted_iota(jnp.int32, x.shape, 1) % HD
    half = HD // 2
    return jnp.where(lane < half, jnp.roll(x, -half, axis=1), jnp.roll(x, half, axis=1))


def rotary(pos, count, plain):
    freq = theta ** (-2.0 * jnp.arange(HD // 2, dtype=F32) / HD)
    angles = pos.astype(F32)[:, None] * freq[None, :]
    cos, sin = jnp.cos(angles), jnp.sin(angles)
    rows = pos.shape[0]
    c = jnp.tile(jnp.concatenate([cos, cos], axis=1), (1, count))
    s = jnp.tile(jnp.concatenate([-sin, sin], axis=1), (1, count))
    return (
        jnp.concatenate([c, jnp.ones((rows, plain), F32)], axis=1),
        jnp.concatenate([s, jnp.zeros((rows, plain), F32)], axis=1),
    )


def inverse_rms(x):
    return lax.rsqrt(jnp.mean(x * x, axis=-1, keepdims=True) + eps)


def norm_back(x, inv, gain, grad):
    scaled = grad * gain
    gain_grad = jnp.sum(grad * x * inv, axis=0)
    return gain_grad, inv * scaled - x * inv**3 * jnp.mean(scaled * x, axis=-1, keepdims=True)


def shards(nf, nz, nt, hidden_in, segments, positions, attn_gain, query_weight, kv_weight,
           out_weight, mlp_gain, gate_up_weight, down_weight, cotangent):
    rows, d = hidden_in.shape[1:]
    heads = query_weight.shape[1] // HD
    kvh = kv_weight.shape[1] // (2 * HD)
    groups = heads // kvh
    dq, dkv = heads * HD, 2 * kvh * HD
    ff = down_weight.shape[1]
    span = rows * nz // 2
    back = min(nz - 1, -(-(span - 1) // rows))
    x = hidden_in.reshape(rows, d).astype(F32)
    pos = positions.reshape(rows)
    top = cotangent.reshape(rows, d)

    ctab, stab = rotary(pos, heads + kvh, kvh * HD)
    r1 = inverse_rms(x)
    head_cols = -(-(dq + dkv) // 256) * 256
    n1, q, kvw, p, att, gains, wall, wgu, wd = attend(
        hidden_in.reshape(rows, d), pos[:, None], ctab[:, :dq], stab[:, :dq],
        jnp.stack([attn_gain, mlp_gain]),
        jnp.concatenate([query_weight, kv_weight, out_weight], axis=1),
        gate_up_weight.reshape(-1, 2 * ff), down_weight,
        nf, nz, nt, back, heads, kvh, head_cols, 2,
    )
    gains = jnp.transpose(gains, (1, 0, 2)).reshape(2, d).astype(F32)
    gain1, gain2 = gains[0], gains[1]
    wall = wall.reshape(d, -1)
    wqkv, wo = wall[:, : dq + dkv], wall[:, dq + dkv :]
    wgu = wgu.reshape(d, 2 * ff)
    wd = wd.reshape(d, ff)
    mid = x + dot(att, wo, 1, 0)
    r2 = inverse_rms(mid)
    n2 = (mid * r2 * gain2).astype(BF)
    gu = dot(n2, wgu, 1, 0)
    gate, up = gu[:, :ff], gu[:, ff:]
    sig = jax.nn.sigmoid(gate)
    hidden = (gate * sig * up).astype(BF)
    gh = dot(top, wd, 1, 0)
    ggu = jnp.concatenate(
        [gh * up * sig * (1.0 + gate * (1.0 - sig)), gh * gate * sig], axis=1
    ).astype(BF)
    part = jnp.concatenate([dot(hidden, wd, 1, 1), dot(ggu, wgu, 1, 1)], axis=1).astype(BF)
    n = nf * nz
    down_grad = dot(top, hidden, 0, 0).astype(BF).reshape(nf, nz, d // n, ff)
    gu_grad = dot(n2, ggu, 0, 0).astype(BF).reshape(nf, nz, d // n, 2 * ff)
    summed, gu_grad, down_grad = tp_sum(
        part.reshape(nt, rows // nt, 2 * d), gu_grad, down_grad, nf, nt, 3
    )
    summed = summed.reshape(rows, 2 * d).astype(F32)
    block_out = (mid + summed[:, :d]).astype(BF).reshape(1, rows, d)
    mlp_gain_grad, grad_norm = norm_back(mid, r2, gain2, summed[:, d:])
    grad_mid = top.astype(F32) + grad_norm
    grad_mid_b = grad_mid.astype(BF)
    go = dot(grad_mid_b, wo, 1, 1).astype(BF)

    grad_q, grad_kv, s1, s2 = attend_back(
        q, kvw, p, att, go, gu_grad, down_grad, nz, nt, back, heads, groups, 4
    )
    grads = jnp.concatenate([grad_q, grad_kv.reshape(rows, dkv).astype(F32)], axis=1)
    grads = (grads * ctab - swap_halves(grads) * stab).astype(BF)
    dw = jnp.concatenate([dot(n1, grads, 0, 0), dot(att, grad_mid_b, 0, 0)], axis=1)
    grad_n1 = dot(grads, wqkv, 1, 1)
    attn_gain_grad, grad_in = norm_back(x, r1, gain1, grad_n1)
    input_grad = (grad_mid + grad_in).reshape(1, rows, d)
    gain_grads = jnp.transpose(
        jnp.stack([attn_gain_grad, mlp_gain_grad]).reshape(2, n, d // n), (1, 0, 2)
    )
    out, gout, o1, o2 = last_sum(
        dw.astype(BF).reshape(n, d // n, -1), gain_grads, s1, s2, nf, nz, nt, 5
    )
    local_d = d // nf
    out = out.reshape(local_d, -1).astype(F32)
    gout = jnp.transpose(gout, (1, 0, 2)).reshape(2, local_d)
    return (
        block_out,
        input_grad,
        gout[0],
        out[:, :dq],
        out[:, dq : dq + dkv],
        out[:, dq + dkv :],
        gout[1],
        o1.reshape(local_d, 2, ff).astype(F32),
        o2.reshape(local_d, ff).astype(F32),
    )


def solution(mesh):
    sizes = mesh.shape
    return jax.shard_map(
        functools.partial(shards, sizes["fsdp"], sizes["ctx"], sizes["tp"]),
        mesh=mesh,
        in_specs=(
            P("fsdp", "ctx", None), P("fsdp", "ctx"), P("fsdp", "ctx"), P("fsdp"),
            P("fsdp", None), P("fsdp", None), P("fsdp", None), P("fsdp"),
            P("fsdp", None, "tp"), P("fsdp", "tp"), P("fsdp", "ctx", None),
        ),
        out_specs=(
            P("fsdp", "ctx", None), P("fsdp", "ctx", None), P("fsdp"),
            P("fsdp", None), P("fsdp", None), P("fsdp", None), P("fsdp"),
            P("fsdp", None, "tp"), P("fsdp", "tp"),
        ),
        check_vma=False,
    )
```

```python
import functools

import jax
import jax.numpy as jnp
from jax import lax
from jax.experimental import pallas as pl
from jax.experimental.pallas import tpu as pltpu
from jax.sharding import PartitionSpec as P

HD = 64
eps = 1e-05
theta = 100000.0
BF = jnp.bfloat16
F32 = jnp.float32
MESH = pl.DeviceIdType.MESH
VM = pl.BlockSpec(memory_space=pltpu.VMEM)


def dot(a, b, ca, cb):
    return lax.dot_general(a, b, (((ca,), (cb,)), ((), ())), preferred_element_type=F32)


def greet(peers):
    barrier = pltpu.get_barrier_semaphore()
    for peer in peers:
        pl.semaphore_signal(barrier, inc=1, device_id=peer, device_id_type=MESH)
    pl.semaphore_wait(barrier, len(peers))


def ring(axis, count, offset):
    return lax.rem(lax.axis_index(axis) + (offset + count), count)


def remote(src, dst, send, recv, device):
    copy = pltpu.make_async_remote_copy(
        src_ref=src, dst_ref=dst, send_sem=send, recv_sem=recv,
        device_id=device, device_id_type=MESH,
    )
    copy.start()
    return copy


def local(src, dst, sem):
    copy = pltpu.make_async_copy(src, dst, sem)
    copy.start()
    return copy


def finish(copies):
    for copy in copies:
        copy.wait()


def across(nt):
    return [{"tp": ring("tp", nt, o)} for o in range(1, nt)]


def partner():
    t = lax.axis_index("tp")
    return {"tp": t + 1 - 2 * lax.rem(t, 2)}


def attend_kernel(nf, nz, nt, back, heads, kvh, head_cols, *refs):
    x_ref, pos_ref, c_ref, s_ref, gain_ref, w_ref, gu_ref, dn_ref = refs[:8]
    n1_ref, q_ref, kvw_ref, p_ref, att_ref, fgain, fw, fgu, fdn = refs[8:17]
    ysend, yrecv, own, psend, precv, ksend, krecv, fsend, frecv = refs[17:]
    rows, d = x_ref.shape
    dq, dkv, dk = heads * HD, 2 * kvh * HD, kvh * HD
    groups = heads // kvh
    f = lax.axis_index("fsdp")
    core = lax.rem(lax.axis_index("tp"), 2)
    mate = partner()
    greet(
        [{"ctx": ring("ctx", nz, o)} for o in range(1, nz)]
        + [{"fsdp": ring("fsdp", nf, o)} for o in range(1, nf)]
        + [mate]
    )
    h1 = head_cols // 2
    h2 = (w_ref.shape[1] - head_cols) // 2
    first = pl.ds(pl.multiple_of(core * h1, 128), h1)
    second = pl.ds(pl.multiple_of(head_cols + core * h2, 128), h2)
    plans = [
        (gain_ref, fgain.at[f]),
        (w_ref.at[:, first], fw.at[f, :, first]),
        (w_ref.at[:, second], fw.at[f, :, second]),
        (dn_ref, fdn.at[f]),
        (gu_ref, fgu.at[f]),
    ]
    sent = [
        [
            remote(src, dst, ysend.at[i, o], yrecv.at[i, o], {"fsdp": ring("fsdp", nf, o)})
            for o in range(1, nf)
        ]
        for i, (src, dst) in enumerate(plans)
    ]
    mine = [
        local(src, dst.at[f], own.at[i])
        for i, (src, dst) in enumerate(
            ((gain_ref, fgain), (w_ref, fw), (dn_ref, fdn), (gu_ref, fgu))
        )
    ]

    def pass_on(i, k, columns):
        out = []
        for o in range(1, nf):
            sent[i][o - 1].wait()
            part = fw.at[ring("fsdp", nf, -o), :, columns]
            out.append(remote(part, part, psend.at[k, o], precv.at[k, o], mate))
        return out

    x = x_ref[...].astype(F32)
    normed = x * lax.rsqrt(jnp.mean(x * x, axis=1, keepdims=True) + eps)
    r = lax.broadcasted_iota(jnp.int32, (dq, dq), 0)
    c = lax.broadcasted_iota(jnp.int32, (dq, dq), 1)
    half = HD // 2
    lane = lax.rem(c, HD)
    perm = jnp.where(r == jnp.where(lane < half, c + half, c - half), 1.0, 0.0).astype(BF)
    finish(mine)
    finish(sent[0])
    finish(pass_on(1, 0, first))
    gain = jnp.concatenate([fgain[i, 0:1, :] for i in range(nf)], axis=1).astype(F32)
    n1 = (normed * gain).astype(BF)
    n1_ref[...] = n1
    w = fw[:, :, : dq + dkv].reshape(d, dq + dkv)
    wq, wk = w[:, :dq], w[:, dq : dq + dk]
    ct, st = c_ref[...], s_ref[...]
    k = dot(n1, wk, 1, 0) * ct[:, :dk] + dot(
        n1, dot(wk, perm[:dk, :dk], 1, 0).astype(BF), 1, 0
    ) * st[:, :dk]
    v = dot(n1, w[:, dq + dk :], 1, 0)
    kvw_ref[back] = jnp.concatenate([k, v], axis=1).astype(BF)
    hr = rows // 2
    block = pl.ds(pl.multiple_of(core * hr, hr), hr)
    kcopies = [
        remote(kvw_ref.at[back, block], kvw_ref.at[back - o, block], ksend.at[o], krecv.at[o],
               {"ctx": ring("ctx", nz, o)})
        for o in range(1, back + 1)
    ]
    q = dot(n1, wq, 1, 0) * ct + dot(n1, dot(wq, perm, 1, 0).astype(BF), 1, 0) * st
    q_ref[...] = (q.astype(BF).astype(F32) * HD ** (-0.5)).astype(BF)
    window = (back + 1) * rows
    jj = lax.broadcasted_iota(jnp.int32, (rows, window), 1) - back * rows
    ii = lax.broadcasted_iota(jnp.int32, (rows, window), 0)
    visible = (jj <= ii) & (jj >= ii - pos_ref[...])
    bias = jnp.where(visible, 0.0, -1e30)
    shared = []
    for o in range(1, back + 1):
        kcopies[o - 1].wait()
        part = kvw_ref.at[back - o, block]
        shared.append(remote(part, part, fsend.at[o], frecv.at[o], mate))
    finish(shared)
    kvw = kvw_ref[...].reshape(window, dkv)
    outs = []
    late = []
    for h in range(heads):
        if h == heads // 2:
            late = pass_on(2, 1, second)
        g = h // groups
        key = kvw[:, g * HD : (g + 1) * HD]
        value = kvw[:, (kvh + g) * HD : (kvh + g + 1) * HD]
        s = dot(q_ref[:, h * HD : (h + 1) * HD], key, 1, 1) + bias
        e = jnp.exp(s - jnp.max(s, axis=1, keepdims=True))
        p = (e * (1.0 / jnp.sum(e, axis=1, keepdims=True))).astype(BF)
        p_ref[h] = p
        outs.append(dot(p, value, 1, 0).astype(BF))
    att_ref[...] = jnp.concatenate(outs, axis=1)
    finish(late)
    finish(sent[3])
    finish(sent[4])


def attend(x, pos, ct, st, gains, w, gu, dn, nf, nz, nt, back, heads, kvh, head_cols, cid):
    rows, d = x.shape
    window = (back + 1) * rows
    sems = pltpu.SemaphoreType.DMA
    shape = jax.ShapeDtypeStruct
    return pl.pallas_call(
        functools.partial(attend_kernel, nf, nz, nt, back, heads, kvh, head_cols),
        out_shape=[
            shape((rows, d), BF),
            shape((rows, heads * HD), BF),
            shape((back + 1, rows, 2 * kvh * HD), BF),
            shape((heads, rows, window), BF),
            shape((rows, heads * HD), BF),
        ]
        + [shape((nf,) + a.shape, a.dtype) for a in (gains, w, gu, dn)],
        in_specs=[VM] * 8,
        out_specs=[VM] * 9,
        scratch_shapes=[
            sems((5, nf)), sems((5, nf)), sems((4,)), sems((2, nf)), sems((2, nf)),
            sems((back + 1,)), sems((back + 1,)), sems((back + 1,)), sems((back + 1,)),
        ],
        compiler_params=pltpu.CompilerParams(collective_id=cid, has_side_effects=True),
        name="attend",
    )(x, pos, ct, st, gains, w, gu, dn)


def tp_sum_kernel(nf, nt, x_ref, g1_ref, g2_ref, out_ref, o1_ref, o2_ref, buf, piece, b1, b2,
                  send, recv, gsend, grecv, own, ysend, yrecv):
    me = lax.axis_index("tp")
    f = lax.axis_index("fsdp")
    greet(across(nt) + [{"fsdp": ring("fsdp", nf, o)} for o in range(1, nf)])
    copies = [
        remote(x_ref.at[ring("tp", nt, o)], buf.at[o], send.at[o], recv.at[o],
               {"tp": ring("tp", nt, o)})
        for o in range(1, nt)
    ]
    side = [
        remote(src.at[ring("fsdp", nf, o)], dst.at[o], ysend.at[i, o], yrecv.at[i, o],
               {"fsdp": ring("fsdp", nf, o)})
        for i, (src, dst) in enumerate(((g1_ref, b1), (g2_ref, b2)))
        for o in range(1, nf)
    ]
    total = x_ref[me].astype(F32)
    for o in range(1, nt):
        copies[o - 1].wait()
        total = total + buf[o].astype(F32)
    piece[...] = total.astype(BF)
    copies = [
        remote(piece, out_ref.at[me], gsend.at[o], grecv.at[o], {"tp": ring("tp", nt, o)})
        for o in range(1, nt)
    ]
    local(piece, out_ref.at[me], own).wait()
    finish(side)
    for src, dst, out in ((g1_ref, b1, o1_ref), (g2_ref, b2, o2_ref)):
        total = src[f].astype(F32)
        for o in range(1, nf):
            total = total + dst[o].astype(F32)
        out[...] = total.astype(BF)
    finish(copies)


def tp_sum(x, g1, g2, nf, nt, cid):
    sems = pltpu.SemaphoreType.DMA
    shape = jax.ShapeDtypeStruct
    return pl.pallas_call(
        functools.partial(tp_sum_kernel, nf, nt),
        out_shape=[shape(x.shape, BF), shape(g1.shape[1:], BF), shape(g2.shape[1:], BF)],
        in_specs=[VM] * 3,
        out_specs=[VM] * 3,
        scratch_shapes=[
            pltpu.VMEM(x.shape, BF), pltpu.VMEM(x.shape[1:], BF),
            pltpu.VMEM(g1.shape, BF), pltpu.VMEM(g2.shape, BF),
            sems((nt,)), sems((nt,)), sems((nt,)), sems((nt,)), sems(()),
            sems((2, nf)), sems((2, nf)),
        ],
        compiler_params=pltpu.CompilerParams(collective_id=cid, has_side_effects=True),
        name="tp_sum",
    )(x, g1, g2)


def grid_offsets(nf, nz):
    return [(a, b) for a in range(nf) for b in range(nz) if (a, b) != (0, 0)]


def grid_peer(nf, nz, a, b):
    return {"fsdp": ring("fsdp", nf, a), "ctx": ring("ctx", nz, b)}


def attend_back_kernel(nz, nt, back, heads, groups, *refs):
    q_ref, kvw_ref, p_ref, att_ref, go_ref, g1_ref, g2_ref = refs[:7]
    dq_ref, dkv_ref, s1_ref, s2_ref = refs[7:11]
    dw_buf, rk_buf, piece, b1, b2, ssem, rsem, own, ksend, krecv, tsend, trecv = refs[11:]
    rows = q_ref.shape[0]
    kvh = heads // groups
    greet([{"ctx": ring("ctx", nz, o)} for o in range(1, nz)] + across(nt))
    me = lax.axis_index("ctx")
    copies = [
        remote(src.at[ring("ctx", nz, o)], buf.at[o], ssem.at[i, o], rsem.at[i, o],
               {"ctx": ring("ctx", nz, o)})
        for i, (src, buf) in enumerate(((g1_ref, b1), (g2_ref, b2)))
        for o in range(1, nz)
    ]
    window = (back + 1) * rows
    kvw = kvw_ref[...].reshape(window, kvw_ref.shape[2])
    dks, dvs, dqs = [], [], []
    for g in range(kvh):
        key = kvw[:, g * HD : (g + 1) * HD]
        value = kvw[:, (kvh + g) * HD : (kvh + g + 1) * HD]
        dk = jnp.zeros((window, HD), F32)
        dv = jnp.zeros((window, HD), F32)
        for h in range(g * groups, (g + 1) * groups):
            q = q_ref[:, h * HD : (h + 1) * HD]
            go = go_ref[:, h * HD : (h + 1) * HD]
            att = att_ref[:, h * HD : (h + 1) * HD]
            delta = jnp.sum(go.astype(F32) * att.astype(F32), axis=1, keepdims=True)
            p = p_ref[h]
            ds = (p.astype(F32) * (dot(go, value, 1, 1) - delta)).astype(BF)
            dv = dv + dot(p, go, 0, 0)
            dk = dk + dot(ds, q, 0, 0)
            dqs.append(dot(ds, key, 1, 0))
        dks.append(dk)
        dvs.append(dv)
    dkv = jnp.concatenate(dks + dvs, axis=1)
    quarter = rows // nt
    t = lax.axis_index("tp")
    block = pl.ds(pl.multiple_of(t * quarter, quarter), quarter)
    dw_buf[...] = dkv.reshape(back + 1, rows, 2 * kvh * HD).astype(BF)
    kcopies = [
        remote(dw_buf.at[back - o, block], rk_buf.at[o - 1], ksend.at[o], krecv.at[o],
               {"ctx": ring("ctx", nz, -o)})
        for o in range(1, back + 1)
    ]
    dq_ref[...] = jnp.concatenate(dqs, axis=1) * HD ** (-0.5)
    total = dw_buf[back, block].astype(F32)
    for o in range(back):
        kcopies[o].wait()
        total = total + rk_buf[o].astype(F32)
    piece[...] = total.astype(BF)
    tcopies = [
        remote(piece, dkv_ref.at[t], tsend.at[o], trecv.at[o], {"tp": ring("tp", nt, o)})
        for o in range(1, nt)
    ]
    local(piece, dkv_ref.at[t], own).wait()
    finish(copies)
    for src, buf, out in ((g1_ref, b1, s1_ref), (g2_ref, b2, s2_ref)):
        total = src[me].astype(F32)
        for o in range(1, nz):
            total = total + buf[o].astype(F32)
        out[...] = total.astype(BF)
    finish(tcopies)


def attend_back(q, kvw, p, att, go, g1, g2, nz, nt, back, heads, groups, cid):
    rows = q.shape[0]
    sems = pltpu.SemaphoreType.DMA
    quarter = rows // nt
    return pl.pallas_call(
        functools.partial(attend_back_kernel, nz, nt, back, heads, groups),
        out_shape=[
            jax.ShapeDtypeStruct(q.shape, F32),
            jax.ShapeDtypeStruct((nt, quarter, kvw.shape[2]), BF),
            jax.ShapeDtypeStruct(g1.shape[1:], BF),
            jax.ShapeDtypeStruct(g2.shape[1:], BF),
        ],
        in_specs=[VM] * 7,
        out_specs=[VM] * 4,
        scratch_shapes=[
            pltpu.VMEM(kvw.shape, BF), pltpu.VMEM((back, quarter, kvw.shape[2]), BF),
            pltpu.VMEM((quarter, kvw.shape[2]), BF),
            pltpu.VMEM(g1.shape, BF), pltpu.VMEM(g2.shape, BF),
            sems((2, nz)), sems((2, nz)), sems(()), sems((back + 1,)), sems((back + 1,)),
            sems((nt,)), sems((nt,)),
        ],
        compiler_params=pltpu.CompilerParams(collective_id=cid, has_side_effects=True),
        name="attend_back",
    )(q, kvw, p, att, go, g1, g2)


def last_sum_kernel(nf, nz, nt, *refs):
    w_ref, v_ref, s1_ref, s2_ref, out_ref, vout_ref, o1_ref, o2_ref = refs[:8]
    wy, wmid, wz, vbuf, piece, vpiece = refs[8:14]
    ysend, yrecv, zsend, zrecv, vsend, vrecv, own, gsend, grecv, rsend, rrecv, tsend, trecv = refs[14:]
    offsets = grid_offsets(nf, nz)
    z = lax.axis_index("ctx")
    f = lax.axis_index("fsdp")
    t = lax.axis_index("tp")
    cols = piece.shape[1]
    columns = pl.ds(pl.multiple_of(t * cols, cols), cols)
    greet([grid_peer(nf, nz, a, b) for a, b in offsets] + across(nt))
    steps = [
        remote(w_ref.at[ring("fsdp", nf, o), :, :, columns], wy.at[o], ysend.at[o], yrecv.at[o],
               {"fsdp": ring("fsdp", nf, o)})
        for o in range(1, nf)
    ]
    mine = [
        local(w_ref.at[f, :, :, columns], wy.at[0], own.at[0]),
        local(s1_ref, o1_ref.at[z], own.at[1]),
        local(s2_ref, o2_ref.at[z], own.at[2]),
    ]
    vcopies = []
    for a, b in offsets:
        target = ring("fsdp", nf, a) * nz + ring("ctx", nz, b)
        slot = a * nz + b
        vcopies.append(
            remote(v_ref.at[target], vbuf.at[slot], vsend.at[slot], vrecv.at[slot],
                   grid_peer(nf, nz, a, b))
        )
    both = [(d, i, ref) for d in (0, 1) for i, ref in enumerate((o1_ref, o2_ref))]

    def inside(index):
        return (index >= 0) & (index < nz)

    def handle(d, i, ref, k, index, device):
        part = ref.at[index]
        return pltpu.make_async_remote_copy(
            src_ref=part, dst_ref=part, send_sem=rsend.at[d, i, k], recv_sem=rrecv.at[d, i, k],
            device_id={"ctx": device}, device_id_type=MESH,
        )

    def relay(k, act):
        for d, i, ref in both:
            way = 1 - 2 * d

            @pl.when(inside(z + way) & inside(z - way * k))
            def _(d=d, i=i, ref=ref, way=way):
                copy = handle(d, i, ref, k, z - way * k, z + way)
                if act == "start":
                    copy.start()
                else:
                    copy.wait_send()

    def arrive(k):
        for d, i, ref in both:
            way = 1 - 2 * d

            @pl.when(inside(z - way * (k + 1)))
            def _(d=d, i=i, ref=ref, way=way):
                handle(d, i, ref, k, z - way * (k + 1), ring("ctx", nz, 1)).wait_recv()

    finish(mine)
    relay(0, "start")
    finish(steps)
    total = wy[0].astype(F32)
    for o in range(1, nf):
        total = total + wy[o].astype(F32)
    wmid[...] = total.astype(BF)
    steps = [
        remote(wmid.at[ring("ctx", nz, o)], wz.at[o], zsend.at[o], zrecv.at[o],
               {"ctx": ring("ctx", nz, o)})
        for o in range(1, nz)
    ]
    arrive(0)
    if nz > 2:
        relay(1, "start")
    finish(vcopies)
    total = v_ref[f * nz + z]
    for i in range(1, nf * nz):
        total = total + vbuf[i]
    vpiece[...] = total
    finish(steps)
    total = wmid[z].astype(F32)
    for o in range(1, nz):
        total = total + wz[o].astype(F32)
    piece[...] = total.astype(BF)
    late = []
    for i, (src, dst) in enumerate(
        ((piece, out_ref.at[z, :, columns]), (vpiece, vout_ref.at[z]))
    ):
        for o in range(1, nz):
            late.append(
                remote(src, dst, gsend.at[i, o], grecv.at[i, o], {"ctx": ring("ctx", nz, o)})
            )
        local(src, dst, own.at[i]).wait()
    for k in range(1, nz - 1):
        arrive(k)
        if k + 1 < nz - 1:
            relay(k + 1, "start")
    finish(late)
    part = out_ref.at[:, :, columns]
    hops = [
        remote(part, part, tsend.at[2 * o], trecv.at[2 * o], {"tp": ring("tp", nt, 2 * o)})
        for o in range(1, nt // 2)
    ]
    swaps = [remote(part, part, tsend.at[0], trecv.at[0], partner())]
    for o in range(1, nt // 2):
        hops[o - 1].wait()
        theirs = lax.rem(t + (nt - 2 * o), nt)
        got = out_ref.at[:, :, pl.ds(pl.multiple_of(theirs * cols, cols), cols)]
        swaps.append(remote(got, got, tsend.at[2 * o + 1], trecv.at[2 * o + 1], partner()))
    finish(swaps)
    for k in range(nz - 1):
        relay(k, "end")


def last_sum(w, v, s1, s2, nf, nz, nt, cid):
    sems = pltpu.SemaphoreType.DMA
    rows, cols = w.shape[2:]
    part = cols // nt
    n = nf * nz
    return pl.pallas_call(
        functools.partial(last_sum_kernel, nf, nz, nt),
        out_shape=[
            jax.ShapeDtypeStruct((nz, rows, cols), BF),
            jax.ShapeDtypeStruct((nz,) + v.shape[1:], F32),
            jax.ShapeDtypeStruct((nz,) + s1.shape, BF),
            jax.ShapeDtypeStruct((nz,) + s2.shape, BF),
        ],
        in_specs=[VM] * 4,
        out_specs=[VM] * 4,
        scratch_shapes=[
            pltpu.VMEM((nf, nz, rows, part), BF), pltpu.VMEM((nz, rows, part), BF),
            pltpu.VMEM((nz, rows, part), BF), pltpu.VMEM(v.shape, F32),
            pltpu.VMEM((rows, part), BF), pltpu.VMEM(v.shape[1:], F32),
            sems((nf,)), sems((nf,)), sems((nz,)), sems((nz,)), sems((n,)), sems((n,)),
            sems((3,)), sems((2, nz)), sems((2, nz)), sems((2, 2, nz)), sems((2, 2, nz)),
            sems((nt,)), sems((nt,)),
        ],
        compiler_params=pltpu.CompilerParams(collective_id=cid, has_side_effects=True),
        name="last_sum",
    )(w, v, s1, s2)


def swap_halves(x):
    width = x.shape[1]
    lane = lax.broadcasted_iota(jnp.int32, x.shape, 1) % HD
    half = HD // 2
    return jnp.where(lane < half, jnp.roll(x, -half, axis=1), jnp.roll(x, half, axis=1))


def rotary(pos, count, plain):
    freq = theta ** (-2.0 * jnp.arange(HD // 2, dtype=F32) / HD)
    angles = pos.astype(F32)[:, None] * freq[None, :]
    cos, sin = jnp.cos(angles), jnp.sin(angles)
    rows = pos.shape[0]
    c = jnp.tile(jnp.concatenate([cos, cos], axis=1), (1, count))
    s = jnp.tile(jnp.concatenate([-sin, sin], axis=1), (1, count))
    return (
        jnp.concatenate([c, jnp.ones((rows, plain), F32)], axis=1),
        jnp.concatenate([s, jnp.zeros((rows, plain), F32)], axis=1),
    )


def inverse_rms(x):
    return lax.rsqrt(jnp.mean(x * x, axis=-1, keepdims=True) + eps)


def norm_back(x, inv, gain, grad):
    scaled = grad * gain
    gain_grad = jnp.sum(grad * x * inv, axis=0)
    return gain_grad, inv * scaled - x * inv**3 * jnp.mean(scaled * x, axis=-1, keepdims=True)


def shards(nf, nz, nt, hidden_in, segments, positions, attn_gain, query_weight, kv_weight,
           out_weight, mlp_gain, gate_up_weight, down_weight, cotangent):
    rows, d = hidden_in.shape[1:]
    heads = query_weight.shape[1] // HD
    kvh = kv_weight.shape[1] // (2 * HD)
    groups = heads // kvh
    dq, dkv = heads * HD, 2 * kvh * HD
    ff = down_weight.shape[1]
    span = rows * nz // 2
    back = min(nz - 1, -(-(span - 1) // rows))
    x = hidden_in.reshape(rows, d).astype(F32)
    pos = positions.reshape(rows)
    top = cotangent.reshape(rows, d)

    ctab, stab = rotary(pos, heads + kvh, kvh * HD)
    r1 = inverse_rms(x)
    head_cols = -(-(dq + dkv) // 256) * 256
    n1, q, kvw, p, att, gains, wall, wgu, wd = attend(
        hidden_in.reshape(rows, d), pos[:, None], ctab[:, :dq], stab[:, :dq],
        jnp.stack([attn_gain, mlp_gain]),
        jnp.concatenate([query_weight, kv_weight, out_weight], axis=1),
        gate_up_weight.reshape(-1, 2 * ff), down_weight,
        nf, nz, nt, back, heads, kvh, head_cols, 2,
    )
    gains = jnp.transpose(gains, (1, 0, 2)).reshape(2, d).astype(F32)
    gain1, gain2 = gains[0], gains[1]
    wall = wall.reshape(d, -1)
    wqkv, wo = wall[:, : dq + dkv], wall[:, dq + dkv :]
    wgu = wgu.reshape(d, 2 * ff)
    wd = wd.reshape(d, ff)
    mid = x + dot(att, wo, 1, 0)
    r2 = inverse_rms(mid)
    n2 = (mid * r2 * gain2).astype(BF)
    gu = dot(n2, wgu, 1, 0)
    gate, up = gu[:, :ff], gu[:, ff:]
    sig = jax.nn.sigmoid(gate)
    hidden = (gate * sig * up).astype(BF)
    gh = dot(top, wd, 1, 0)
    ggu = jnp.concatenate(
        [gh * up * sig * (1.0 + gate * (1.0 - sig)), gh * gate * sig], axis=1
    ).astype(BF)
    part = jnp.concatenate([dot(hidden, wd, 1, 1), dot(ggu, wgu, 1, 1)], axis=1).astype(BF)
    n = nf * nz
    down_grad = dot(top, hidden, 0, 0).astype(BF).reshape(nf, nz, d // n, ff)
    gu_grad = dot(n2, ggu, 0, 0).astype(BF).reshape(nf, nz, d // n, 2 * ff)
    summed, gu_grad, down_grad = tp_sum(
        part.reshape(nt, rows // nt, 2 * d), gu_grad, down_grad, nf, nt, 3
    )
    summed = summed.reshape(rows, 2 * d).astype(F32)
    block_out = (mid + summed[:, :d]).astype(BF).reshape(1, rows, d)
    mlp_gain_grad, grad_norm = norm_back(mid, r2, gain2, summed[:, d:])
    grad_mid = top.astype(F32) + grad_norm
    grad_mid_b = grad_mid.astype(BF)
    go = dot(grad_mid_b, wo, 1, 1).astype(BF)

    grad_q, grad_kv, s1, s2 = attend_back(
        q, kvw, p, att, go, gu_grad, down_grad, nz, nt, back, heads, groups, 4
    )
    grads = jnp.concatenate([grad_q, grad_kv.reshape(rows, dkv).astype(F32)], axis=1)
    grads = (grads * ctab - swap_halves(grads) * stab).astype(BF)
    dw = jnp.concatenate([dot(n1, grads, 0, 0), dot(att, grad_mid_b, 0, 0)], axis=1)
    grad_n1 = dot(grads, wqkv, 1, 1)
    attn_gain_grad, grad_in = norm_back(x, r1, gain1, grad_n1)
    input_grad = (grad_mid + grad_in).reshape(1, rows, d)
    gain_grads = jnp.transpose(
        jnp.stack([attn_gain_grad, mlp_gain_grad]).reshape(2, n, d // n), (1, 0, 2)
    )
    out, gout, o1, o2 = last_sum(
        dw.astype(BF).reshape(nf, nz, d // n, -1), gain_grads, s1, s2, nf, nz, nt, 5
    )
    local_d = d // nf
    out = out.reshape(local_d, -1).astype(F32)
    gout = jnp.transpose(gout, (1, 0, 2)).reshape(2, local_d)
    return (
        block_out,
        input_grad,
        gout[0],
        out[:, :dq],
        out[:, dq : dq + dkv],
        out[:, dq + dkv :],
        gout[1],
        o1.reshape(local_d, 2, ff).astype(F32),
        o2.reshape(local_d, ff).astype(F32),
    )


def solution(mesh):
    sizes = mesh.shape
    return jax.shard_map(
        functools.partial(shards, sizes["fsdp"], sizes["ctx"], sizes["tp"]),
        mesh=mesh,
        in_specs=(
            P("fsdp", "ctx", None), P("fsdp", "ctx"), P("fsdp", "ctx"), P("fsdp"),
            P("fsdp", None), P("fsdp", None), P("fsdp", None), P("fsdp"),
            P("fsdp", None, "tp"), P("fsdp", "tp"), P("fsdp", "ctx", None),
        ),
        out_specs=(
            P("fsdp", "ctx", None), P("fsdp", "ctx", None), P("fsdp"),
            P("fsdp", None), P("fsdp", None), P("fsdp", None), P("fsdp"),
            P("fsdp", None, "tp"), P("fsdp", "tp"),
        ),
        check_vma=False,
    )
```
